256 devices in a mesh: tensor: 8 (over z), expert: 32 (over x, y, core).
Axes of the slice: x: 4, y: 4, z: 8, core: 2. Of those that a mesh axis runs over, the one named last changes fastest.
Arguments:
- queries: bfloat16 [768, 64, 576], P('expert', 'tensor'), may hold values from -200 to 200
- latent_cache_rows: bfloat16 [768, 24, 576], P('expert'), may hold values from -5 to 5
- lengths: int32 [768], P('expert'), may hold values from 6 to 24, as said below
- value_up_weight: bfloat16 [64, 512, 128], P('tensor'), may hold values from -0.25 to 0.25
- w_output: bfloat16 [8192, 7168], P('tensor', 'expert'), may hold values from -0.0625 to 0.0625
- residual: bfloat16 [768, 7168], P(None, 'expert'), may hold values from -3 to 3
- norm_gain: float32 [7168], replicated, may hold values from 0.1 to 1.9
- routes: int32 [768, 8], replicated, may hold values from 0 to 31, as said below
- gate_values: float32 [768, 8], replicated, may hold values from 0.05 to 0.5
- capacity: int32 [32], replicated, may hold values from 224 to 448, as said below
- w_gate: bfloat16 [32, 7168, 2048], P('expert', None, 'tensor'), may hold values from -0.0625 to 0.0625
- w_up: bfloat16 [32, 7168, 2048], P('expert', None, 'tensor'), may hold values from -0.0625 to 0.0625
- w_down: bfloat16 [32, 2048, 7168], P('expert', 'tensor'), may hold values from -0.125 to 0.125
Outputs:
- layer_output: bfloat16 [768, 7168], P('tensor', 'expert')
The draws below stay inside these ranges and needn't reach their ends.
Inputs may be any that keep to these rules, and one draw needn't show every extreme that they name: Row r attends over its first lengths[r] cache slots; some row fills all 24 in every draw. `routes`: each row names 8 different experts. Some expert has capacity 448 in every draw.
All inputs are finite; a program needn't handle non-finite values.
Results may differ from the reference program's by a relative error of at most 0.0073.
Values may be sent and summed in bfloat16 or wider, within the bound.
No kernel may reach another device: no remote copies, remote signals or barrier semaphores. Data moves between devices by JAX's collectives and lax.ppermute only.
A program may use at most 128 MiB of HBM per device.

```python
import math
import jax
import jax.numpy as jnp
from jax import lax

D = 7168
QUERY_HEADS = 64
LATENT_CHANNELS = 512
ROTARY_CHANNELS = 64
NOPE = 128
VALUE_CHANNELS = 128
MOE_FF = 2048
TOP_K = 8
CACHE = 24
TOKEN_ROWS = 768
SPECIALIST_COUNT = 32
BUFFER_PLACES = 448


def attention_pair(key):
    starting_key = jax.random.fold_in(key, 11)
    cache_key, query_key = jax.random.split(starting_key, 2)
    channel_total = LATENT_CHANNELS + ROTARY_CHANNELS
    latent_cache_rows = jnp.clip(jax.random.normal(cache_key, (TOKEN_ROWS, CACHE, channel_total), jnp.float32), -5.0, 5.0)
    queries = jnp.clip(jax.random.normal(query_key, (TOKEN_ROWS, QUERY_HEADS, channel_total), jnp.float32), -5.0, 5.0)
    return (latent_cache_rows, queries)


def draw_queries(key, part):
    return attention_pair(key)[1].astype(jnp.bfloat16)


def draw_latent_cache_rows(key, part):
    return attention_pair(key)[0].astype(jnp.bfloat16)


def draw_lengths(key, part):
    length_key, longest_key = jax.random.split(jax.random.fold_in(key, 31))
    drawn_len = jax.random.randint(length_key, (TOKEN_ROWS,), CACHE // 4, CACHE + 1)
    longest_row = jax.random.randint(longest_key, (), 0, TOKEN_ROWS)
    return drawn_len.at[longest_row].set(CACHE).astype(jnp.int32)


def route_pair(key):
    starting_key = jax.random.fold_in(key, 23)
    popular_key, extra_score_key, routing_score_key, limit_seed = jax.random.split(starting_key, 4)
    specialist_numbers = jnp.arange(SPECIALIST_COUNT, dtype=jnp.int32)
    favoured_specialist = jax.random.randint(popular_key, (), 0, SPECIALIST_COUNT)
    expert_extra_score = jax.random.randint(extra_score_key, (SPECIALIST_COUNT,), 0, 3) * 2 ** 19
    expert_extra_score = jnp.where(specialist_numbers == favoured_specialist, 2 ** 23, expert_extra_score)
    noise_score = jax.random.randint(routing_score_key, (TOKEN_ROWS, SPECIALIST_COUNT), 0, 2 ** 20)
    ranked_experts = (noise_score + expert_extra_score[None, :]) * SPECIALIST_COUNT + specialist_numbers[None, :]
    _, selected_specialists = lax.top_k(ranked_experts, TOP_K)
    specialist_limits = jax.random.randint(limit_seed, (SPECIALIST_COUNT,), BUFFER_PLACES // 2, BUFFER_PLACES + 1)
    specialist_limits = jnp.where(specialist_numbers == favoured_specialist, BUFFER_PLACES, specialist_limits)
    return (selected_specialists.astype(jnp.int32), specialist_limits.astype(jnp.int32))


def draw_routes(key, part):
    return route_pair(key)[0]


def draw_capacity(key, part):
    return route_pair(key)[1]


def level_of(key, extent, pieces, low, largest):
    def one(axis_at, shards_of):
        draws = jax.random.uniform(jax.random.fold_in(jax.random.fold_in(key, 6), axis_at), (shards_of,), jnp.float32, low / len(pieces), largest / len(pieces))
        return jnp.repeat(jnp.exp(draws), extent[axis_at] // shards_of).reshape((-1,) + (1,) * (len(extent) - axis_at - 1))

    gain = one(*pieces[0])
    for cut in pieces[1:]:
        gain = gain * one(*cut)
    return gain


def noise(stream_key, dims, deviation, bound, cuts=(), held_as=jnp.bfloat16):
    entries = jax.random.normal(stream_key, dims, jnp.float32) * deviation
    if len(cuts) > 0:
        entries = level_of(stream_key, dims, cuts, -0.22, 0.18) * entries
    return jnp.clip(entries, min=-bound, max=bound).astype(held_as)


def setup_inputs(seed: int = 0) -> dict:
    key_of = jax.random.split(jax.random.key(seed), 14)
    return {
        "queries": draw_queries(jax.random.fold_in(key_of[13], 71), 0),
        "latent_cache_rows": draw_latent_cache_rows(jax.random.fold_in(key_of[13], 71), 0),
        "lengths": draw_lengths(jax.random.fold_in(key_of[13], 71), 0),
        "value_up_weight": noise(key_of[3], (QUERY_HEADS, LATENT_CHANNELS, VALUE_CHANNELS), LATENT_CHANNELS ** -0.5, 0.25, ((0, 8),)),
        "w_output": noise(key_of[4], (QUERY_HEADS * VALUE_CHANNELS, D), (QUERY_HEADS * VALUE_CHANNELS) ** -0.5, 0.0625, ((0, 8), (1, 32))),
        "residual": noise(key_of[5], (TOKEN_ROWS, D), 0.5, 3.0, ((1, 32),)),
        "norm_gain": jnp.clip(1.0 + 0.18 * jax.random.normal(key_of[6], (D,), jnp.float32), 0.1, 1.9),
        "routes": draw_routes(jax.random.fold_in(key_of[13], 71), 0),
        "gate_values": jnp.clip(jnp.exp(jax.random.uniform(key_of[8], (TOKEN_ROWS, TOP_K), jnp.float32, math.log(0.05), math.log(0.5))), 0.05, 0.5),
        "capacity": draw_capacity(jax.random.fold_in(key_of[13], 71), 0),
        "w_gate": noise(key_of[10], (SPECIALIST_COUNT, D, MOE_FF), D ** -0.5, 0.0625, ((0, 32), (2, 8))),
        "w_up": noise(key_of[11], (SPECIALIST_COUNT, D, MOE_FF), D ** -0.5, 0.0625, ((0, 32), (2, 8))),
        "w_down": noise(key_of[12], (SPECIALIST_COUNT, MOE_FF, D), MOE_FF ** -0.5, 0.125, ((0, 32), (1, 8))),
    }


epsilon = 1e-06

def slot_tables(routes, gate_values, capacity):
    experts_total = capacity.shape[0]
    flat_ids = routes.reshape(-1).astype(jnp.int32)
    one_hot = (flat_ids[:, None] == jnp.arange(experts_total, dtype=jnp.int32)[None, :]).astype(jnp.int32)
    earlier = jnp.cumsum(one_hot, axis=0) - one_hot
    position = lax.optimization_barrier(jnp.sum(earlier * one_hot, axis=1))
    limit_of = lax.optimization_barrier(jnp.sum(one_hot * capacity[None, :], axis=1))
    kept_pair = position < limit_of
    target = jnp.where(kept_pair, flat_ids * BUFFER_PLACES + position, experts_total * BUFFER_PLACES).astype(jnp.int32)
    row_index = (jnp.arange(flat_ids.shape[0], dtype=jnp.int32) // TOP_K).astype(jnp.int32)
    slot_row = jnp.full((experts_total * BUFFER_PLACES + 1,), TOKEN_ROWS, jnp.int32).at[target].set(row_index)
    slot_row = slot_row[:experts_total * BUFFER_PLACES].reshape(experts_total, BUFFER_PLACES)
    slot_gate = jnp.zeros((experts_total * BUFFER_PLACES + 1,), jnp.float32).at[target].set(gate_values.reshape(-1))
    slot_gate = slot_gate[:experts_total * BUFFER_PLACES].reshape(experts_total, BUFFER_PLACES)
    return (slot_row, slot_gate)

def reference(queries, latent_cache_rows, lengths, value_up_weight, w_output, residual, norm_gain, routes, gate_values, capacity, w_gate, w_up, w_down):
    softmax_scale = (NOPE + ROTARY_CHANNELS) ** (-0.5)
    scores = jnp.einsum('rhc,rpc->rhp', queries.astype(jnp.float32), latent_cache_rows.astype(jnp.float32)) * softmax_scale
    live_slot = jnp.arange(CACHE, dtype=jnp.int32)[None, None, :] < lengths[:, None, None]
    scores = jnp.where(live_slot, scores, -jnp.inf)
    row_peak = lax.optimization_barrier(jnp.max(scores, axis=-1, keepdims=True))
    weight_exp = jnp.exp(scores - row_peak)
    attention_probs = (weight_exp / lax.optimization_barrier(jnp.sum(weight_exp, axis=-1, keepdims=True))).astype(jnp.bfloat16)
    latent_rows = jnp.einsum('onq,oqv->onv', attention_probs.astype(jnp.float32), latent_cache_rows[:, :, :LATENT_CHANNELS].astype(jnp.float32)).astype(jnp.bfloat16)
    head_out = jnp.einsum('rhc,hcv->rhv', latent_rows.astype(jnp.float32), value_up_weight.astype(jnp.float32)).astype(jnp.bfloat16)
    head_out = head_out.reshape(TOKEN_ROWS, QUERY_HEADS * VALUE_CHANNELS)
    attention = jnp.dot(head_out, w_output, preferred_element_type=jnp.float32)
    stream = (residual.astype(jnp.float32) + attention).astype(jnp.bfloat16)
    as_float = stream.astype(jnp.float32)
    normed = (as_float * lax.rsqrt(lax.optimization_barrier(jnp.mean(as_float * as_float, axis=-1, keepdims=True)) + epsilon) * norm_gain).astype(jnp.bfloat16)
    slot_row, slot_gate = slot_tables(routes, gate_values, capacity)
    normed_pad = jnp.concatenate([normed, jnp.zeros((1, D), jnp.bfloat16)], axis=0)

    def one_expert(accumulated, expert_item):
        slot_rows, slot_weights, gate_proj, up_proj, down_proj = expert_item
        inputs = normed_pad[slot_rows]
        gate_pre = jnp.dot(inputs, gate_proj, preferred_element_type=jnp.float32)
        up_pre = jnp.dot(inputs, up_proj, preferred_element_type=jnp.float32)
        activated = (jax.nn.silu(gate_pre) * up_pre).astype(jnp.bfloat16)
        produced = jnp.dot(activated, down_proj, preferred_element_type=jnp.float32)
        accumulated = accumulated.at[slot_rows].add(slot_weights[:, None] * produced, mode='drop')
        return (accumulated, None)
    combined, _ = lax.scan(one_expert, jnp.zeros((TOKEN_ROWS, D), jnp.float32), (slot_row, slot_gate, w_gate, w_up, w_down))
    return (stream.astype(jnp.float32) + combined).astype(jnp.bfloat16)
```

```python
import jax
import jax.numpy as jnp
from jax import lax
from jax.sharding import PartitionSpec as P

ROTARY_CHANNELS = 64
NOPE = 128
SIDE = 4
CORES = 2

epsilon = 1e-06


def place(x, y, core):
    return (x * SIDE + y) * CORES + core


def ring_groups():
    along_y = [[place(x, y, 0) for y in range(SIDE)] for x in range(SIDE)]
    along_x = [[place(x, y, 0) for x in range(SIDE)] for y in range(SIDE)]
    along_y1 = [[place(x, y, 1) for y in range(SIDE)] for x in range(SIDE)]
    along_x1 = [[place(x, y, 1) for x in range(SIDE)] for y in range(SIDE)]
    inner = along_y + along_x1
    outer = along_x + along_y1
    pairs = [[place(x, y, 0), place(x, y, 1)] for x in range(SIDE) for y in range(SIDE)]
    return inner, outer, pairs


INNER, OUTER, PAIRS = ring_groups()


def exchange(blocks, groups):
    return lax.all_to_all(blocks, "expert", 0, 0, axis_index_groups=groups, tiled=True)


def spread(block, groups, count):
    return exchange(jnp.broadcast_to(block[None], (count,) + block.shape), groups)


def gather_plane(block):
    block = spread(block, INNER, SIDE)
    block = spread(block, OUTER, SIDE)
    return spread(block, PAIRS, CORES)


def add_blocks(blocks):
    return jnp.sum(blocks.astype(jnp.float32), axis=0)


def plane_order(table):
    tail = table.shape[1:]
    cube = table.reshape((SIDE, SIDE, CORES) + tail)
    return jnp.stack([cube[:, :, 0], jnp.swapaxes(cube[:, :, 1], 0, 1)])


def row_order(table):
    return jnp.stack([table[0], jnp.swapaxes(table[1], 0, 1)], axis=2)


def shards(
    queries,
    latent_cache_rows,
    lengths,
    value_up_weight,
    w_output,
    residual,
    norm_gain,
    routes,
    gate_values,
    capacity,
    w_gate,
    w_up,
    w_down,
):
    latent_width = value_up_weight.shape[1]
    softmax_scale = (NOPE + ROTARY_CHANNELS) ** (-0.5)
    scores = (
        jnp.einsum("rhc,rpc->rhp", queries, latent_cache_rows, preferred_element_type=jnp.float32)
        * softmax_scale
    )
    slot_total = latent_cache_rows.shape[1]
    live_slot = lax.broadcasted_iota(jnp.int32, (1, 1, slot_total), 2) < lengths[:, None, None]
    scores = jnp.where(live_slot, scores, -jnp.inf)
    row_peak = jnp.max(scores, axis=-1, keepdims=True)
    weight_exp = jnp.exp(scores - row_peak)
    attention_probs = (weight_exp / jnp.sum(weight_exp, axis=-1, keepdims=True)).astype(
        jnp.bfloat16
    )
    latent_rows = jnp.einsum(
        "onq,oqv->onv",
        attention_probs,
        latent_cache_rows[:, :, :latent_width],
        preferred_element_type=jnp.float32,
    ).astype(jnp.bfloat16)
    head_out = jnp.einsum(
        "rhc,hcv->rhv", latent_rows, value_up_weight, preferred_element_type=jnp.float32
    ).astype(jnp.bfloat16)
    head_rows = head_out.reshape(head_out.shape[0], -1)

    expert = lax.axis_index("expert")
    layer = lax.axis_index("tensor")
    layers = lax.axis_size("tensor")
    row_total, column_width = residual.shape
    own_rows = row_total // layers
    model_width = norm_gain.shape[0]
    hidden = w_gate.shape[2]

    named = routes == expert
    member = jnp.any(named, axis=1)
    gate_of = jnp.sum(jnp.where(named, gate_values, 0.0), axis=1)
    earlier = jnp.arange(row_total)[:, None] > jnp.arange(row_total)[None, :]
    position = jnp.dot(
        earlier.astype(jnp.bfloat16),
        member.astype(jnp.bfloat16),
        preferred_element_type=jnp.float32,
    )
    limit = capacity[expert].astype(jnp.float32)
    row_weight = jnp.where(position < limit, gate_of, 0.0)

    gate_up = jnp.concatenate([w_gate[0], w_up[0]], axis=1)
    gate_up = plane_order(gate_up.reshape(-1, column_width, 2 * hidden))
    gate_up = gate_up.reshape(model_width, 2 * hidden)
    down = plane_order(w_down[0].T.reshape(-1, column_width, hidden))
    down = down.reshape(model_width, hidden)
    gain = plane_order(norm_gain.reshape(-1, column_width)).reshape(model_width, 1)

    heads = gather_plane(head_rows)
    partial_out = jnp.dot(
        heads.reshape(row_total, -1), w_output, preferred_element_type=jnp.float32
    )
    partial_out = partial_out.reshape(CORES, SIDE, SIDE, -1, column_width)
    partial_out = row_order(partial_out).reshape(layers, own_rows, column_width)
    attention = add_blocks(
        lax.all_to_all(partial_out.astype(jnp.bfloat16), "tensor", 0, 0, tiled=True)
    )
    own_residual = lax.dynamic_slice_in_dim(residual, layer * own_rows, own_rows, 0)
    stream = (own_residual.astype(jnp.float32) + attention).astype(jnp.bfloat16)
    columns = lax.all_to_all(
        jnp.broadcast_to(stream[None], (layers,) + stream.shape), "tensor", 0, 0, tiled=True
    )
    columns = columns.reshape(row_total, column_width).T

    full = gather_plane(columns).reshape(model_width, row_total)
    as_float = full.astype(jnp.float32)
    scale = lax.rsqrt(jnp.mean(as_float * as_float, axis=0, keepdims=True) + epsilon)
    normed = (as_float * scale * gain).astype(jnp.bfloat16)
    pre = lax.dot_general(
        gate_up, normed, (((0,), (0,)), ((), ())), preferred_element_type=jnp.float32
    )
    activated = (jax.nn.silu(pre[:hidden]) * pre[hidden:]).astype(jnp.bfloat16)
    produced = jnp.dot(down, activated, preferred_element_type=jnp.float32)
    weighted = (produced * row_weight[None, :]).astype(jnp.bfloat16)

    parts = weighted.reshape(CORES, SIDE, SIDE, column_width, row_total)
    parts = add_blocks(exchange(parts, PAIRS)).astype(jnp.bfloat16)
    parts = add_blocks(exchange(parts, OUTER)).astype(jnp.bfloat16)
    parts = add_blocks(exchange(parts, INNER)).astype(jnp.bfloat16)
    parts = parts.T.reshape(layers, own_rows, column_width)
    combined = add_blocks(lax.all_to_all(parts, "tensor", 0, 0, tiled=True))
    return (stream.astype(jnp.float32) + combined).astype(jnp.bfloat16)


def solution(mesh):
    in_specs = (
        P("expert", "tensor", None),
        P("expert", None, None),
        P("expert"),
        P("tensor", None, None),
        P("tensor", "expert"),
        P(None, "expert"),
        P(),
        P(),
        P(),
        P(),
        P("expert", None, "tensor"),
        P("expert", None, "tensor"),
        P("expert", "tensor", None),
    )
    out_specs = P("tensor", "expert")
    return jax.shard_map(shards, mesh=mesh, in_specs=in_specs, out_specs=out_specs, check_vma=False)
```

```python
import jax
import jax.numpy as jnp
from jax import lax
from jax.experimental import pallas as pl
from jax.experimental.pallas import tpu as pltpu
from jax.sharding import PartitionSpec as P

ROTARY_CHANNELS = 64
NOPE = 128
SIDE = 4
CORES = 2

epsilon = 1e-06


def place(x, y, core):
    return (x * SIDE + y) * CORES + core


def ring_groups():
    along_y = [[place(x, y, 0) for y in range(SIDE)] for x in range(SIDE)]
    along_x = [[place(x, y, 0) for x in range(SIDE)] for y in range(SIDE)]
    along_y1 = [[place(x, y, 1) for y in range(SIDE)] for x in range(SIDE)]
    along_x1 = [[place(x, y, 1) for x in range(SIDE)] for y in range(SIDE)]
    inner = along_y + along_x1
    outer = along_x + along_y1
    pairs = [[place(x, y, 0), place(x, y, 1)] for x in range(SIDE) for y in range(SIDE)]
    return inner, outer, pairs


INNER, OUTER, PAIRS = ring_groups()


def exchange(blocks, groups):
    return lax.all_to_all(blocks, "expert", 0, 0, axis_index_groups=groups, tiled=True)


def spread(block, groups, count):
    return exchange(jnp.broadcast_to(block[None], (count,) + block.shape), groups)


def gather_plane(block):
    block = spread(block, INNER, SIDE)
    block = spread(block, OUTER, SIDE)
    return spread(block, PAIRS, CORES)


def shift(block, groups, step):
    pairs = []
    for ring in groups:
        size = len(ring)
        pairs += [(ring[i], ring[(i + step) % size]) for i in range(size)]
    return lax.ppermute(block, "expert", pairs)


def add_blocks(blocks):
    return jnp.sum(blocks.astype(jnp.float32), axis=0)


def row_order(table):
    return jnp.stack([table[0], jnp.swapaxes(table[1], 0, 1)], axis=2)


def plane_tables(expert):
    x, y, core = expert // (SIDE * CORES), (expert // CORES) % SIDE, expert % CORES
    a = jnp.where(core == 0, x, y)
    b = jnp.where(core == 0, y, x)
    step = jnp.arange(SIDE, dtype=jnp.int32)

    def index(c, outer, inner):
        outer = outer % SIDE
        inner = inner % SIDE
        even = (outer * SIDE + inner) * CORES
        odd = (inner * SIDE + outer) * CORES + 1
        return jnp.where(c == 0, even, odd).astype(jnp.int32)

    k, j = step[:, None], step[None, :]
    back = SIDE - k, SIDE - j
    own_in = index(core, a + back[0], b + back[1])
    mate_in = index(1 - core, b + back[0], a + back[1])
    own_out = index(core, a + k, b + j)
    mate_out = index(1 - core, b + k, a + j)
    return own_in, mate_in, own_out, mate_out


def in_body(table, x_ref, w_ref, acc_in, sq_in, acc_ref, sq_ref):
    step = pl.program_id(0)

    @pl.when(step == 0)
    def _():
        acc_ref[...] = acc_in[...]
        sq_ref[...] = sq_in[...]

    block = x_ref[0]
    acc_ref[...] += jnp.dot(w_ref[0], block, preferred_element_type=jnp.float32)
    wide = block.astype(jnp.float32)
    folded = (wide * wide).reshape(-1, 8, wide.shape[1])
    sq_ref[...] += jnp.sum(folded, axis=0)


def project_in(k, table, blocks, weights, acc, squares):
    count, depth, rows = blocks.shape
    units = weights.shape[1]
    keep = pl.BlockSpec((units, rows), lambda i, t: (0, 0))
    keep_sq = pl.BlockSpec(squares.shape, lambda i, t: (0, 0))
    return pl.pallas_call(
        in_body,
        out_shape=(
            jax.ShapeDtypeStruct(acc.shape, jnp.float32),
            jax.ShapeDtypeStruct(squares.shape, jnp.float32),
        ),
        grid_spec=pltpu.PrefetchScalarGridSpec(
            num_scalar_prefetch=1,
            grid=(count,),
            in_specs=[
                pl.BlockSpec((1, depth, rows), lambda i, t: (i, 0, 0)),
                pl.BlockSpec((1, units, depth), lambda i, t: (t[k, i], 0, 0)),
                keep,
                keep_sq,
            ],
            out_specs=(keep, keep_sq),
        ),
        compiler_params=pltpu.CompilerParams(vmem_limit_bytes=24 * 2**20),
        cost_estimate=pl.CostEstimate(
            flops=2 * count * depth * rows * units,
            bytes_accessed=2 * count * depth * (rows + units),
            transcendentals=0,
        ),
    )(table, blocks, weights, acc, squares)


def out_body(table, act_ref, scale_ref, w_ref, out_ref):
    made = jnp.dot(w_ref[0], act_ref[...], preferred_element_type=jnp.float32)
    out_ref[0] = (made * scale_ref[...]).astype(out_ref.dtype)


def out_add_body(table, act_ref, scale_ref, w_ref, mate_ref, out_ref):
    made = jnp.dot(w_ref[0], act_ref[...], preferred_element_type=jnp.float32)
    made = made * scale_ref[...] + mate_ref[0].astype(jnp.float32)
    out_ref[0] = made.astype(out_ref.dtype)


def project_out(k, table, act, scale, weights, mate=None):
    units, rows = act.shape
    depth = weights.shape[1]
    block = pl.BlockSpec((1, depth, rows), lambda i, t: (i, 0, 0))
    in_specs = [
        pl.BlockSpec((units, rows), lambda i, t: (0, 0)),
        pl.BlockSpec((1, rows), lambda i, t: (0, 0)),
        pl.BlockSpec((1, depth, units), lambda i, t: (t[k, i], 0, 0)),
    ]
    args = [table, act, scale, weights]
    if mate is not None:
        in_specs.append(block)
        args.append(mate)
    return pl.pallas_call(
        out_body if mate is None else out_add_body,
        out_shape=jax.ShapeDtypeStruct((SIDE, depth, rows), jnp.bfloat16),
        grid_spec=pltpu.PrefetchScalarGridSpec(
            num_scalar_prefetch=1, grid=(SIDE,), in_specs=in_specs, out_specs=block
        ),
        compiler_params=pltpu.CompilerParams(vmem_limit_bytes=16 * 2**20),
        cost_estimate=pl.CostEstimate(
            flops=2 * SIDE * depth * rows * units,
            bytes_accessed=2 * SIDE * depth * (rows + units),
            transcendentals=0,
        ),
    )(*args)


ORDER = (2, 1, 3)


def shards(
    queries,
    latent_cache_rows,
    lengths,
    value_up_weight,
    w_output,
    residual,
    norm_gain,
    routes,
    gate_values,
    capacity,
    w_gate,
    w_up,
    w_down,
):
    latent_width = value_up_weight.shape[1]
    softmax_scale = (NOPE + ROTARY_CHANNELS) ** (-0.5)
    scores = (
        jnp.einsum("rhc,rpc->rhp", queries, latent_cache_rows, preferred_element_type=jnp.float32)
        * softmax_scale
    )
    slot_total = latent_cache_rows.shape[1]
    live_slot = lax.broadcasted_iota(jnp.int32, (1, 1, slot_total), 2) < lengths[:, None, None]
    scores = jnp.where(live_slot, scores, -jnp.inf)
    row_peak = jnp.max(scores, axis=-1, keepdims=True)
    weight_exp = jnp.exp(scores - row_peak)
    attention_probs = (weight_exp / jnp.sum(weight_exp, axis=-1, keepdims=True)).astype(
        jnp.bfloat16
    )
    latent_rows = jnp.einsum(
        "onq,oqv->onv",
        attention_probs,
        latent_cache_rows[:, :, :latent_width],
        preferred_element_type=jnp.float32,
    ).astype(jnp.bfloat16)
    head_out = jnp.einsum(
        "rhc,hcv->rhv", latent_rows, value_up_weight, preferred_element_type=jnp.float32
    ).astype(jnp.bfloat16)
    head_rows = head_out.reshape(head_out.shape[0], -1)

    expert = lax.axis_index("expert")
    layer = lax.axis_index("tensor")
    layers = lax.axis_size("tensor")
    row_total, column_width = residual.shape
    own_rows = row_total // layers
    model_width = norm_gain.shape[0]
    hidden = w_gate.shape[2]

    named = routes == expert
    member = jnp.any(named, axis=1)
    gate_of = jnp.sum(jnp.where(named, gate_values, 0.0), axis=1)
    earlier = jnp.arange(row_total)[:, None] > jnp.arange(row_total)[None, :]
    position = jnp.dot(
        earlier.astype(jnp.bfloat16),
        member.astype(jnp.bfloat16),
        preferred_element_type=jnp.float32,
    )
    limit = capacity[expert].astype(jnp.float32)
    row_weight = jnp.where(position < limit, gate_of, 0.0)

    gain = norm_gain.reshape(-1, column_width)[:, None, :]

    def turned(table):
        blocks = jnp.swapaxes(table.reshape(-1, column_width, hidden), 1, 2)
        return (blocks.astype(jnp.float32) * gain).astype(jnp.bfloat16)

    gate_up = jnp.concatenate([turned(w_gate[0]), turned(w_up[0])], axis=1)
    down = w_down[0].T.reshape(-1, column_width, hidden)
    own_in, mate_in, own_out, mate_out = plane_tables(expert)

    heads = gather_plane(head_rows)
    partial_out = jnp.dot(
        heads.reshape(row_total, -1), w_output, preferred_element_type=jnp.float32
    )
    partial_out = partial_out.reshape(CORES, SIDE, SIDE, -1, column_width)
    partial_out = row_order(partial_out).reshape(layers, own_rows, column_width)
    attention = add_blocks(
        lax.all_to_all(partial_out.astype(jnp.bfloat16), "tensor", 0, 0, tiled=True)
    )
    own_residual = lax.dynamic_slice_in_dim(residual, layer * own_rows, own_rows, 0)
    stream = (own_residual.astype(jnp.float32) + attention).astype(jnp.bfloat16)
    columns = lax.all_to_all(
        jnp.broadcast_to(stream[None], (layers,) + stream.shape), "tensor", 0, 0, tiled=True
    )
    columns = columns.reshape(row_total, column_width).T

    ring = [columns] + [shift(columns, INNER, k) for k in range(1, SIDE)]
    ring = jnp.stack(ring)
    arrived = {0: ring}
    for k in ORDER:
        arrived[k] = shift(ring, OUTER, k)
    total = jnp.zeros((2 * hidden, row_total), jnp.float32)
    squares = jnp.zeros((8, row_total), jnp.float32)
    for k in (0,) + ORDER:
        mate = shift(arrived[k], PAIRS, 1)
        total, squares = project_in(k, own_in, arrived[k], gate_up, total, squares)
        total, squares = project_in(k, mate_in, mate, gate_up, total, squares)
    mean_square = jnp.sum(squares, axis=0, keepdims=True) / model_width
    pre = total * lax.rsqrt(mean_square + epsilon)
    activated = (jax.nn.silu(pre[:hidden]) * pre[hidden:]).astype(jnp.bfloat16)

    scale = row_weight[None, :]
    sums = []
    for k in ORDER + (0,):
        mate = shift(project_out(k, mate_out, activated, scale, down), PAIRS, 1)
        group = project_out(k, own_out, activated, scale, down, mate)
        sums.append(group if k == 0 else shift(group, OUTER, k))
    parts = add_blocks(jnp.stack(sums)).astype(jnp.bfloat16)
    parts = add_blocks(
        jnp.stack([parts[0]] + [shift(parts[k], INNER, k) for k in range(1, SIDE)])
    ).astype(jnp.bfloat16)
    parts = parts.T.reshape(layers, own_rows, column_width)
    combined = add_blocks(lax.all_to_all(parts, "tensor", 0, 0, tiled=True))
    return (stream.astype(jnp.float32) + combined).astype(jnp.bfloat16)


def solution(mesh):
    in_specs = (
        P("expert", "tensor", None),
        P("expert", None, None),
        P("expert"),
        P("tensor", None, None),
        P("tensor", "expert"),
        P(None, "expert"),
        P(),
        P(),
        P(),
        P(),
        P("expert", None, "tensor"),
        P("expert", None, "tensor"),
        P("expert", "tensor", None),
    )
    out_specs = P("tensor", "expert")
    return jax.shard_map(shards, mesh=mesh, in_specs=in_specs, out_specs=out_specs, check_vma=False)
```

```python
import functools

import jax
import jax.numpy as jnp
from jax import lax
from jax.experimental import pallas as pl
from jax.experimental.pallas import tpu as pltpu
from jax.sharding import PartitionSpec as P

ROTARY_CHANNELS = 64
NOPE = 128
SIDE = 4
CORES = 2

epsilon = 1e-06


def place(x, y, core):
    return (x * SIDE + y) * CORES + core


def ring_groups():
    along_y = [[place(x, y, 0) for y in range(SIDE)] for x in range(SIDE)]
    along_x = [[place(x, y, 0) for x in range(SIDE)] for y in range(SIDE)]
    along_y1 = [[place(x, y, 1) for y in range(SIDE)] for x in range(SIDE)]
    along_x1 = [[place(x, y, 1) for x in range(SIDE)] for y in range(SIDE)]
    inner = along_y + along_x1
    outer = along_x + along_y1
    pairs = [[place(x, y, 0), place(x, y, 1)] for x in range(SIDE) for y in range(SIDE)]
    return inner, outer, pairs


INNER, OUTER, PAIRS = ring_groups()


def exchange(blocks, groups):
    return lax.all_to_all(blocks, "expert", 0, 0, axis_index_groups=groups, tiled=True)


def spread(block, groups, count):
    return exchange(jnp.broadcast_to(block[None], (count,) + block.shape), groups)


def gather_plane(block):
    block = spread(block, INNER, SIDE)
    block = spread(block, OUTER, SIDE)
    return spread(block, PAIRS, CORES)


def shift(block, groups, step):
    pairs = []
    for ring in groups:
        size = len(ring)
        pairs += [(ring[i], ring[(i + step) % size]) for i in range(size)]
    return lax.ppermute(block, "expert", pairs)


def add_blocks(blocks):
    return jnp.sum(blocks.astype(jnp.float32), axis=0)


def row_order(table):
    return jnp.stack([table[0], jnp.swapaxes(table[1], 0, 1)], axis=2)


def plane_tables(expert):
    x, y, core = expert // (SIDE * CORES), (expert // CORES) % SIDE, expert % CORES
    a = jnp.where(core == 0, x, y)
    b = jnp.where(core == 0, y, x)
    step = jnp.arange(SIDE, dtype=jnp.int32)

    def index(c, outer, inner):
        outer = outer % SIDE
        inner = inner % SIDE
        even = (outer * SIDE + inner) * CORES
        odd = (inner * SIDE + outer) * CORES + 1
        return jnp.where(c == 0, even, odd).astype(jnp.int32)

    k, j = step[:, None], step[None, :]
    back = SIDE - k, SIDE - j
    own_in = index(core, a + back[0], b + back[1])
    mate_in = index(1 - core, b + back[0], a + back[1])
    own_out = index(core, a + k, b + j)
    mate_out = index(1 - core, b + k, a + j)
    return own_in, mate_in, own_out, mate_out


def in_body(fresh, table, x_ref, *refs):
    gates, ups, gains = refs[:SIDE], refs[SIDE : 2 * SIDE], refs[2 * SIDE : 3 * SIDE]
    refs = refs[3 * SIDE :]
    acc_ref, sq_ref = refs[-2:]
    half = acc_ref.shape[0] // 2
    for j in range(SIDE):
        wide = x_ref[j].astype(jnp.float32)
        folded = jnp.sum((wide * wide).reshape(-1, 8, wide.shape[1]), axis=0)
        block = (wide * gains[j][0]).astype(jnp.bfloat16)
        gate = jnp.dot(gates[j][0], block, preferred_element_type=jnp.float32)
        up = jnp.dot(ups[j][0], block, preferred_element_type=jnp.float32)
        if j == 0:
            gate_sum, up_sum, square_sum = gate, up, folded
        else:
            gate_sum, up_sum, square_sum = gate_sum + gate, up_sum + up, square_sum + folded
    if not fresh:
        gate_sum += refs[0][:half]
        up_sum += refs[0][half:]
        square_sum += refs[1][...]
    acc_ref[:half] = gate_sum
    acc_ref[half:] = up_sum
    sq_ref[...] = square_sum


ROW_TILE = 256


def project_in(k, table, blocks, gate, up, gain, sums):
    count, depth, rows = blocks.shape
    units = gate.shape[1]
    keep = pl.BlockSpec((2 * units, ROW_TILE), lambda i, t: (0, i))
    keep_sq = pl.BlockSpec((8, ROW_TILE), lambda i, t: (0, i))

    def picked(shape):
        return [
            pl.BlockSpec((1,) + shape, lambda i, t, j=j: (t[k, j], 0, 0)) for j in range(count)
        ]

    in_specs = [pl.BlockSpec((count, depth, ROW_TILE), lambda i, t: (0, 0, i))]
    in_specs += picked((units, depth)) + picked((units, depth)) + picked((depth, 1))
    args = [table, blocks] + [gate] * count + [up] * count + [gain] * count
    if sums is not None:
        in_specs += [keep, keep_sq]
        args += list(sums)
    return pl.pallas_call(
        functools.partial(in_body, sums is None),
        out_shape=(
            jax.ShapeDtypeStruct((2 * units, rows), jnp.float32),
            jax.ShapeDtypeStruct((8, rows), jnp.float32),
        ),
        grid_spec=pltpu.PrefetchScalarGridSpec(
            num_scalar_prefetch=1,
            grid=(rows // ROW_TILE,),
            in_specs=in_specs,
            out_specs=(keep, keep_sq),
        ),
        compiler_params=pltpu.CompilerParams(vmem_limit_bytes=24 * 2**20),
        cost_estimate=pl.CostEstimate(
            flops=4 * count * depth * rows * units,
            bytes_accessed=2 * count * depth * (rows + 2 * units),
            transcendentals=0,
        ),
    )(*args)


def out_body(table, act_ref, scale_ref, w_ref, out_ref):
    made = jnp.dot(w_ref[0], act_ref[...], preferred_element_type=jnp.float32)
    out_ref[0] = (made * scale_ref[...]).astype(out_ref.dtype)


def out_add_body(table, act_ref, scale_ref, w_ref, mate_ref, out_ref):
    made = jnp.dot(w_ref[0], act_ref[...], preferred_element_type=jnp.float32)
    made = made * scale_ref[...] + mate_ref[0].astype(jnp.float32)
    out_ref[0] = made.astype(out_ref.dtype)


def project_out(k, table, act, scale, weights, mate=None):
    units, rows = act.shape
    depth = weights.shape[1]
    block = pl.BlockSpec((1, depth, rows), lambda i, t: (i, 0, 0))
    in_specs = [
        pl.BlockSpec((units, rows), lambda i, t: (0, 0)),
        pl.BlockSpec((1, rows), lambda i, t: (0, 0)),
        pl.BlockSpec((1, depth, units), lambda i, t: (t[k, i], 0, 0)),
    ]
    args = [table, act, scale, weights]
    if mate is not None:
        in_specs.append(block)
        args.append(mate)
    return pl.pallas_call(
        out_body if mate is None else out_add_body,
        out_shape=jax.ShapeDtypeStruct((SIDE, depth, rows), jnp.bfloat16),
        grid_spec=pltpu.PrefetchScalarGridSpec(
            num_scalar_prefetch=1, grid=(SIDE,), in_specs=in_specs, out_specs=block
        ),
        compiler_params=pltpu.CompilerParams(vmem_limit_bytes=16 * 2**20),
        cost_estimate=pl.CostEstimate(
            flops=2 * SIDE * depth * rows * units,
            bytes_accessed=2 * SIDE * depth * (rows + units),
            transcendentals=0,
        ),
    )(*args)


ORDER = (2, 1, 3)


def shards(
    queries,
    latent_cache_rows,
    lengths,
    value_up_weight,
    w_output,
    residual,
    norm_gain,
    routes,
    gate_values,
    capacity,
    w_gate,
    w_up,
    w_down,
):
    latent_width = value_up_weight.shape[1]
    softmax_scale = (NOPE + ROTARY_CHANNELS) ** (-0.5)
    scores = (
        jnp.einsum("rhc,rpc->rhp", queries, latent_cache_rows, preferred_element_type=jnp.float32)
        * softmax_scale
    )
    slot_total = latent_cache_rows.shape[1]
    live_slot = lax.broadcasted_iota(jnp.int32, (1, 1, slot_total), 2) < lengths[:, None, None]
    scores = jnp.where(live_slot, scores, -jnp.inf)
    row_peak = jnp.max(scores, axis=-1, keepdims=True)
    weight_exp = jnp.exp(scores - row_peak)
    attention_probs = (weight_exp / jnp.sum(weight_exp, axis=-1, keepdims=True)).astype(
        jnp.bfloat16
    )
    latent_rows = jnp.einsum(
        "onq,oqv->onv",
        attention_probs,
        latent_cache_rows[:, :, :latent_width],
        preferred_element_type=jnp.float32,
    ).astype(jnp.bfloat16)
    head_out = jnp.einsum(
        "rhc,hcv->rhv", latent_rows, value_up_weight, preferred_element_type=jnp.float32
    ).astype(jnp.bfloat16)
    head_rows = head_out.reshape(head_out.shape[0], -1)

    expert = lax.axis_index("expert")
    layer = lax.axis_index("tensor")
    layers = lax.axis_size("tensor")
    row_total, column_width = residual.shape
    own_rows = row_total // layers
    model_width = norm_gain.shape[0]
    hidden = w_gate.shape[2]

    named = routes == expert
    member = jnp.any(named, axis=1)
    gate_of = jnp.sum(jnp.where(named, gate_values, 0.0), axis=1)
    earlier = jnp.arange(row_total)[:, None] > jnp.arange(row_total)[None, :]
    position = jnp.dot(
        earlier.astype(jnp.bfloat16),
        member.astype(jnp.bfloat16),
        preferred_element_type=jnp.float32,
    )
    limit = capacity[expert].astype(jnp.float32)
    row_weight = jnp.where(position < limit, gate_of, 0.0)

    gain = norm_gain.reshape(-1, column_width, 1)
    gate = jnp.swapaxes(w_gate[0].reshape(-1, column_width, hidden), 1, 2)
    up = jnp.swapaxes(w_up[0].reshape(-1, column_width, hidden), 1, 2)
    down = w_down[0].T.reshape(-1, column_width, hidden)
    own_in, mate_in, own_out, mate_out = plane_tables(expert)

    heads = gather_plane(head_rows)
    partial_out = jnp.dot(
        heads.reshape(row_total, -1), w_output, preferred_element_type=jnp.float32
    )
    partial_out = partial_out.reshape(CORES, SIDE, SIDE, -1, column_width)
    partial_out = row_order(partial_out).reshape(layers, own_rows, column_width)
    parts = lax.all_to_all(partial_out.astype(jnp.bfloat16), "tensor", 0, 0, tiled=True)
    parts, gate, up = lax.optimization_barrier((parts, gate, up))
    attention = add_blocks(parts)
    own_residual = lax.dynamic_slice_in_dim(residual, layer * own_rows, own_rows, 0)
    stream = (own_residual.astype(jnp.float32) + attention).astype(jnp.bfloat16)
    columns = lax.all_to_all(
        jnp.broadcast_to(stream[None], (layers,) + stream.shape), "tensor", 0, 0, tiled=True
    )
    held = columns, down, gain, row_weight, own_in, mate_in, own_out, mate_out
    held = lax.optimization_barrier(held)
    columns, down, gain, row_weight, own_in, mate_in, own_out, mate_out = held
    columns = columns.reshape(row_total, column_width).T

    ring = [columns] + [shift(columns, INNER, k) for k in range(1, SIDE)]
    ring = jnp.stack(ring)
    arrived = {0: ring}
    for k in ORDER:
        arrived[k] = shift(ring, OUTER, k)

    def swap_in(k):
        return shift(arrived[k], PAIRS, 1)

    def add_in(table, k, block, sums):
        return project_in(k, table, block, gate, up, gain, sums)

    mates = {0: swap_in(0)}
    sums = add_in(own_in, 0, ring, None)
    sums = add_in(mate_in, 0, mates[0], sums)
    arrived[2], sums = lax.optimization_barrier((arrived[2], sums))
    mates[2] = swap_in(2)
    sums = add_in(own_in, 2, arrived[2], sums)
    sums = add_in(mate_in, 2, mates[2], sums)
    arrived[1], arrived[3], sums = lax.optimization_barrier((arrived[1], arrived[3], sums))
    mates.update({k: swap_in(k) for k in (1, 3)})
    for k in (1, 3):
        sums = add_in(own_in, k, arrived[k], sums)
    for k in (1, 3):
        sums = add_in(mate_in, k, mates[k], sums)
    total, squares = sums
    mean_square = jnp.sum(squares, axis=0, keepdims=True) / model_width
    pre = total * lax.rsqrt(mean_square + epsilon)
    activated = (jax.nn.silu(pre[:hidden]) * pre[hidden:]).astype(jnp.bfloat16)

    scale = row_weight[None, :]

    def for_mate(k):
        made = project_out(k, mate_out, activated, scale, down)
        return shift(made, PAIRS, 1)

    sums, mates = [], {2: for_mate(2)}
    for k, following in ((2, 1), (1, 3), (3, 0), (0, None)):
        if following is not None:
            mates[following] = for_mate(following)
        group = project_out(k, own_out, activated, scale, down, mates[k])
        if following is None:
            sums.append(group)
        else:
            group, activated = lax.optimization_barrier((group, activated))
            sums.append(shift(group, OUTER, k))
    parts = add_blocks(jnp.stack(sums)).astype(jnp.bfloat16)
    parts = add_blocks(
        jnp.stack([parts[0]] + [shift(parts[k], INNER, k) for k in range(1, SIDE)])
    ).astype(jnp.bfloat16)
    parts = parts.T.reshape(layers, own_rows, column_width)
    combined = add_blocks(lax.all_to_all(parts, "tensor", 0, 0, tiled=True))
    return (stream.astype(jnp.float32) + combined).astype(jnp.bfloat16)


def solution(mesh):
    in_specs = (
        P("expert", "tensor", None),
        P("expert", None, None),
        P("expert"),
        P("tensor", None, None),
        P("tensor", "expert"),
        P(None, "expert"),
        P(),
        P(),
        P(),
        P(),
        P("expert", None, "tensor"),
        P("expert", None, "tensor"),
        P("expert", "tensor", None),
    )
    out_specs = P("tensor", "expert")
    return jax.shard_map(
        shards, mesh=mesh, in_specs=in_specs, out_specs=out_specs, check_vma=False
    )
```

```python
import functools

import jax
import jax.numpy as jnp
from jax import lax
from jax.experimental import pallas as pl
from jax.experimental.pallas import tpu as pltpu
from jax.sharding import PartitionSpec as P

ROTARY_CHANNELS = 64
NOPE = 128
SIDE = 4
CORES = 2

epsilon = 1e-06


def place(x, y, core):
    return (x * SIDE + y) * CORES + core


def ring_groups():
    along_y = [[place(x, y, 0) for y in range(SIDE)] for x in range(SIDE)]
    along_x = [[place(x, y, 0) for x in range(SIDE)] for y in range(SIDE)]
    along_y1 = [[place(x, y, 1) for y in range(SIDE)] for x in range(SIDE)]
    along_x1 = [[place(x, y, 1) for x in range(SIDE)] for y in range(SIDE)]
    inner = along_y + along_x1
    outer = along_x + along_y1
    pairs = [[place(x, y, 0), place(x, y, 1)] for x in range(SIDE) for y in range(SIDE)]
    return inner, outer, pairs


INNER, OUTER, PAIRS = ring_groups()


def exchange(blocks, groups):
    return lax.all_to_all(blocks, "expert", 0, 0, axis_index_groups=groups, tiled=True)


def spread(block, groups, count):
    return exchange(jnp.broadcast_to(block[None], (count,) + block.shape), groups)


def gather_plane(block):
    block = spread(block, INNER, SIDE)
    block = spread(block, OUTER, SIDE)
    return spread(block, PAIRS, CORES)


def shift(block, groups, step):
    pairs = []
    for ring in groups:
        size = len(ring)
        pairs += [(ring[i], ring[(i + step) % size]) for i in range(size)]
    return lax.ppermute(block, "expert", pairs)


def add_blocks(blocks):
    return jnp.sum(blocks.astype(jnp.float32), axis=0)


def row_order(table):
    return jnp.stack([table[0], jnp.swapaxes(table[1], 0, 1)], axis=2)


def plane_tables(expert):
    x, y, core = expert // (SIDE * CORES), (expert // CORES) % SIDE, expert % CORES
    a = jnp.where(core == 0, x, y)
    b = jnp.where(core == 0, y, x)
    step = jnp.arange(SIDE, dtype=jnp.int32)

    def index(c, outer, inner):
        outer = outer % SIDE
        inner = inner % SIDE
        even = (outer * SIDE + inner) * CORES
        odd = (inner * SIDE + outer) * CORES + 1
        return jnp.where(c == 0, even, odd).astype(jnp.int32)

    k, j = step[:, None], step[None, :]
    back = SIDE - k, SIDE - j
    own_in = index(core, a + back[0], b + back[1])
    mate_in = index(1 - core, b + back[0], a + back[1])
    own_out = index(core, a + k, b + j)
    mate_out = index(1 - core, b + k, a + j)
    return own_in, mate_in, own_out, mate_out


def in_body(spots, fresh, table, *refs):
    count = len(spots)
    arrays = 1 + max(a for a, _, _ in spots)
    blocks, refs = refs[:arrays], refs[arrays:]
    gates, ups, gains = refs[:count], refs[count : 2 * count], refs[2 * count : 3 * count]
    refs = refs[3 * count :]
    acc_ref, sq_ref, left, right = refs[-4:]
    half, step = gates[0].shape[1:]
    depth = blocks[0].shape[1]

    @pl.when(pl.program_id(0) == 0)
    def _():
        for c in range(count):
            left[:half, c * step : (c + 1) * step] = gates[c][0]
            left[half:, c * step : (c + 1) * step] = ups[c][0]
            blank = jnp.zeros((step - depth, right.shape[1]), right.dtype)
            right[c * step + depth : (c + 1) * step] = blank

    square_sum = jnp.zeros(sq_ref.shape, jnp.float32) if fresh else refs[1][...]
    for c, (a, row, _) in enumerate(spots):
        wide = blocks[a][row].astype(jnp.float32)
        square_sum += jnp.sum((wide * wide).reshape(-1, 8, wide.shape[1]), axis=0)
        right[c * step : c * step + depth] = (wide * gains[c][0]).astype(right.dtype)
    sq_ref[...] = square_sum
    made = jnp.dot(left[...], right[...], preferred_element_type=jnp.float32)
    acc_ref[...] = made if fresh else made + refs[0][...]


ROW_TILE = 256


def project_in(spots, table, blocks, gate, up, gain, sums):
    count = len(spots)
    depth, rows = blocks[0].shape[1:]
    units, step = gate.shape[1:]
    keep = pl.BlockSpec((2 * units, ROW_TILE), lambda i, t: (0, i))
    keep_sq = pl.BlockSpec((8, ROW_TILE), lambda i, t: (0, i))

    def picked(shape):
        return [
            pl.BlockSpec((1,) + shape, lambda i, t, k=k, j=j: (t[k, j], 0, 0))
            for _, _, (k, j) in spots
        ]

    in_specs = [
        pl.BlockSpec((b.shape[0], depth, ROW_TILE), lambda i, t: (0, 0, i)) for b in blocks
    ]
    in_specs += picked((units, step)) + picked((units, step)) + picked((depth, 1))
    args = [table] + list(blocks) + [gate] * count + [up] * count + [gain] * count
    if sums is not None:
        in_specs += [keep, keep_sq]
        args += list(sums)
    return pl.pallas_call(
        functools.partial(in_body, spots, sums is None),
        out_shape=(
            jax.ShapeDtypeStruct((2 * units, rows), jnp.float32),
            jax.ShapeDtypeStruct((8, rows), jnp.float32),
        ),
        grid_spec=pltpu.PrefetchScalarGridSpec(
            num_scalar_prefetch=1,
            grid=(rows // ROW_TILE,),
            in_specs=in_specs,
            out_specs=(keep, keep_sq),
            scratch_shapes=[
                pltpu.VMEM((2 * units, count * step), jnp.bfloat16),
                pltpu.VMEM((count * step, ROW_TILE), jnp.bfloat16),
            ],
        ),
        compiler_params=pltpu.CompilerParams(vmem_limit_bytes=32 * 2**20),
        cost_estimate=pl.CostEstimate(
            flops=4 * count * depth * rows * units,
            bytes_accessed=2 * count * depth * (rows + 2 * units),
            transcendentals=0,
        ),
    )(*args)


def out_body(table, act_ref, scale_ref, w_ref, out_ref):
    made = jnp.dot(w_ref[0], act_ref[...], preferred_element_type=jnp.float32)
    out_ref[0] = (made * scale_ref[...]).astype(out_ref.dtype)


def out_add_body(table, act_ref, scale_ref, w_ref, mate_ref, far_ref, near_ref):
    made = jnp.dot(w_ref[0], act_ref[...], preferred_element_type=jnp.float32)
    made = made * scale_ref[...] + mate_ref[0].astype(jnp.float32)
    made = made.astype(far_ref.dtype)

    @pl.when(pl.program_id(0) < SIDE - 1)
    def _():
        far_ref[0] = made

    @pl.when(pl.program_id(0) == SIDE - 1)
    def _():
        near_ref[...] = made


def project_out(k, table, act, scale, weights, mate=None):
    units, rows = act.shape
    depth = weights.shape[1]
    block = pl.BlockSpec((1, depth, rows), lambda i, t: (i, 0, 0))
    in_specs = [
        pl.BlockSpec((units, rows), lambda i, t: (0, 0)),
        pl.BlockSpec((1, rows), lambda i, t: (0, 0)),
        pl.BlockSpec((1, depth, units), lambda i, t: (t[k, (i + 1) % SIDE], 0, 0)),
    ]
    args = [table, act, scale, weights]
    if mate is None:
        out_shape = jax.ShapeDtypeStruct((SIDE, depth, rows), jnp.bfloat16)
        out_specs = block
    else:
        in_specs.append(block)
        args.append(mate)
        out_shape = (
            jax.ShapeDtypeStruct((SIDE - 1, depth, rows), jnp.bfloat16),
            jax.ShapeDtypeStruct((depth, rows), jnp.bfloat16),
        )
        out_specs = (
            pl.BlockSpec((1, depth, rows), lambda i, t: (jnp.minimum(i, SIDE - 2), 0, 0)),
            pl.BlockSpec((depth, rows), lambda i, t: (0, 0)),
        )
    return pl.pallas_call(
        out_body if mate is None else out_add_body,
        out_shape=out_shape,
        grid_spec=pltpu.PrefetchScalarGridSpec(
            num_scalar_prefetch=1, grid=(SIDE,), in_specs=in_specs, out_specs=out_specs
        ),
        compiler_params=pltpu.CompilerParams(vmem_limit_bytes=16 * 2**20),
        cost_estimate=pl.CostEstimate(
            flops=2 * SIDE * depth * rows * units,
            bytes_accessed=2 * SIDE * depth * (rows + units),
            transcendentals=0,
        ),
    )(*args)


FAR = (2, 1, 3)
PADDED = 256


def shards(
    queries,
    latent_cache_rows,
    lengths,
    value_up_weight,
    w_output,
    residual,
    norm_gain,
    routes,
    gate_values,
    capacity,
    w_gate,
    w_up,
    w_down,
):
    latent_width = value_up_weight.shape[1]
    softmax_scale = (NOPE + ROTARY_CHANNELS) ** (-0.5)
    scores = (
        jnp.einsum("rhc,rpc->rhp", queries, latent_cache_rows, preferred_element_type=jnp.float32)
        * softmax_scale
    )
    slot_total = latent_cache_rows.shape[1]
    live_slot = lax.broadcasted_iota(jnp.int32, (1, 1, slot_total), 2) < lengths[:, None, None]
    scores = jnp.where(live_slot, scores, -jnp.inf)
    row_peak = jnp.max(scores, axis=-1, keepdims=True)
    weight_exp = jnp.exp(scores - row_peak)
    attention_probs = (weight_exp / jnp.sum(weight_exp, axis=-1, keepdims=True)).astype(
        jnp.bfloat16
    )
    latent_rows = jnp.einsum(
        "onq,oqv->onv",
        attention_probs,
        latent_cache_rows[:, :, :latent_width],
        preferred_element_type=jnp.float32,
    ).astype(jnp.bfloat16)
    head_out = jnp.einsum(
        "rhc,hcv->rhv", latent_rows, value_up_weight, preferred_element_type=jnp.float32
    ).astype(jnp.bfloat16)
    head_rows = head_out.reshape(head_out.shape[0], -1)

    expert = lax.axis_index("expert")
    layer = lax.axis_index("tensor")
    layers = lax.axis_size("tensor")
    row_total, column_width = residual.shape
    own_rows = row_total // layers
    model_width = norm_gain.shape[0]
    hidden = w_gate.shape[2]

    named = routes == expert
    member = jnp.any(named, axis=1)
    gate_of = jnp.sum(jnp.where(named, gate_values, 0.0), axis=1)
    earlier = jnp.arange(row_total)[:, None] > jnp.arange(row_total)[None, :]
    position = jnp.dot(
        earlier.astype(jnp.bfloat16),
        member.astype(jnp.bfloat16),
        preferred_element_type=jnp.float32,
    )
    limit = capacity[expert].astype(jnp.float32)
    row_weight = jnp.where(position < limit, gate_of, 0.0)

    gain = norm_gain.reshape(-1, column_width, 1)

    def turned(table):
        blocks = jnp.swapaxes(table.reshape(-1, column_width, hidden), 1, 2)
        return jnp.pad(blocks, ((0, 0), (0, 0), (0, PADDED - column_width)))

    gate, up = turned(w_gate[0]), turned(w_up[0])
    down = w_down[0].T.reshape(-1, column_width, hidden)
    own_in, mate_in, own_out, mate_out = plane_tables(expert)

    heads = gather_plane(head_rows)
    partial_out = jnp.dot(
        heads.reshape(row_total, -1), w_output, preferred_element_type=jnp.float32
    )
    partial_out = partial_out.reshape(CORES, SIDE, SIDE, -1, column_width)
    partial_out = row_order(partial_out).reshape(layers, own_rows, column_width)
    parts = lax.all_to_all(partial_out.astype(jnp.bfloat16), "tensor", 0, 0, tiled=True)
    parts, gate, up = lax.optimization_barrier((parts, gate, up))
    attention = add_blocks(parts)
    own_residual = lax.dynamic_slice_in_dim(residual, layer * own_rows, own_rows, 0)
    stream = (own_residual.astype(jnp.float32) + attention).astype(jnp.bfloat16)
    columns = lax.all_to_all(
        jnp.broadcast_to(stream[None], (layers,) + stream.shape), "tensor", 0, 0, tiled=True
    )
    held = columns, down, gain, row_weight, own_in, mate_in, own_out, mate_out
    held = lax.optimization_barrier(held)
    columns, down, gain, row_weight, own_in, mate_in, own_out, mate_out = held
    columns = columns.reshape(row_total, column_width).T

    inner = []
    for k in range(1, SIDE):
        inner.append(shift(columns, INNER, k))
    first, second = {}, {}
    for k in FAR:
        first[k] = shift(columns, OUTER, k)
    inner = jnp.stack(inner)
    for k in FAR:
        second[k] = shift(inner, OUTER, k)

    def swap(block):
        return shift(block, PAIRS, 1)

    def add_in(spots, table, blocks, sums):
        return project_in(spots, table, blocks, gate, up, gain, sums)

    here = ((0, 0, (0, 0)),) + tuple((1, j - 1, (0, j)) for j in range(1, SIDE))
    ones = tuple((0, k - 1, (k, 0)) for k in range(1, SIDE))

    def rest(*steps):
        return tuple(
            (a, j - 1, (k, j)) for a, k in enumerate(steps) for j in range(1, SIDE)
        )

    own = [columns[None], inner]
    mate = [swap(columns)[None], swap(inner)]
    sums = add_in(here, own_in, own, None)
    sums = add_in(here, mate_in, mate, sums)
    heads_of = jnp.stack([first[k] for k in range(1, SIDE)])
    heads_of, sums = lax.optimization_barrier((heads_of, sums))
    mate = swap(heads_of)
    sums = add_in(ones, own_in, [heads_of], sums)
    sums = add_in(ones, mate_in, [mate], sums)
    second[2], sums = lax.optimization_barrier((second[2], sums))
    mate = swap(second[2])
    sums = add_in(rest(2), own_in, [second[2]], sums)
    sums = add_in(rest(2), mate_in, [mate], sums)
    second[1], second[3], sums = lax.optimization_barrier((second[1], second[3], sums))
    mate = [swap(second[1]), swap(second[3])]
    sums = add_in(rest(1, 3), own_in, [second[1], second[3]], sums)
    sums = add_in(rest(1, 3), mate_in, mate, sums)
    total, squares = sums
    mean_square = jnp.sum(squares, axis=0, keepdims=True) / model_width
    pre = total * lax.rsqrt(mean_square + epsilon)
    activated = (jax.nn.silu(pre[:hidden]) * pre[hidden:]).astype(jnp.bfloat16)

    scale = row_weight[None, :]

    def for_mate(k):
        made = project_out(k, mate_out, activated, scale, down)
        return shift(made, PAIRS, 1)

    far, near, mates = {}, {}, {2: for_mate(2)}
    for k, following in ((2, 1), (1, 3), (3, 0), (0, None)):
        if following is not None:
            mates[following] = for_mate(following)
        group = project_out(k, own_out, activated, scale, down, mates[k])
        if following is not None:
            far[k], near[k], activated = lax.optimization_barrier((*group, activated))
        else:
            far[k], near[k] = group
    for k in FAR:
        far[k] = shift(far[k], OUTER, k)
    for k in FAR:
        near[k] = shift(near[k], OUTER, k)
    parts = add_blocks(jnp.stack([far[k] for k in range(SIDE)])).astype(jnp.bfloat16)
    around = []
    for k in range(1, SIDE):
        around.append(shift(parts[k - 1], INNER, k))
    parts = add_blocks(jnp.stack([near[k] for k in range(SIDE)]))
    parts = (parts + add_blocks(jnp.stack(around))).astype(jnp.bfloat16)
    parts = parts.T.reshape(layers, own_rows, column_width)
    combined = add_blocks(lax.all_to_all(parts, "tensor", 0, 0, tiled=True))
    return (stream.astype(jnp.float32) + combined).astype(jnp.bfloat16)


def solution(mesh):
    in_specs = (
        P("expert", "tensor", None),
        P("expert", None, None),
        P("expert"),
        P("tensor", None, None),
        P("tensor", "expert"),
        P(None, "expert"),
        P(),
        P(),
        P(),
        P(),
        P("expert", None, "tensor"),
        P("expert", None, "tensor"),
        P("expert", "tensor", None),
    )
    out_specs = P("tensor", "expert")
    return jax.shard_map(
        shards, mesh=mesh, in_specs=in_specs, out_specs=out_specs, check_vma=False
    )
```

```python
import functools

import jax
import jax.numpy as jnp
from jax import lax
from jax.experimental import pallas as pl
from jax.experimental.pallas import tpu as pltpu
from jax.sharding import PartitionSpec as P

ROTARY_CHANNELS = 64
NOPE = 128
SIDE = 4
CORES = 2

epsilon = 1e-06


def place(x, y, core):
    return (x * SIDE + y) * CORES + core


def ring_groups():
    along_y = [[place(x, y, 0) for y in range(SIDE)] for x in range(SIDE)]
    along_x = [[place(x, y, 0) for x in range(SIDE)] for y in range(SIDE)]
    along_y1 = [[place(x, y, 1) for y in range(SIDE)] for x in range(SIDE)]
    along_x1 = [[place(x, y, 1) for x in range(SIDE)] for y in range(SIDE)]
    inner = along_y + along_x1
    outer = along_x + along_y1
    pairs = [[place(x, y, 0), place(x, y, 1)] for x in range(SIDE) for y in range(SIDE)]
    return inner, outer, pairs


INNER, OUTER, PAIRS = ring_groups()


def exchange(blocks, groups):
    return lax.all_to_all(blocks, "expert", 0, 0, axis_index_groups=groups, tiled=True)


def spread(block, groups, count):
    return exchange(jnp.broadcast_to(block[None], (count,) + block.shape), groups)


def gather_plane(block):
    block = spread(block, INNER, SIDE)
    block = spread(block, OUTER, SIDE)
    return spread(block, PAIRS, CORES)


def shift(block, groups, step):
    pairs = []
    for ring in groups:
        size = len(ring)
        pairs += [(ring[i], ring[(i + step) % size]) for i in range(size)]
    return lax.ppermute(block, "expert", pairs)


def add_blocks(blocks):
    return jnp.sum(blocks.astype(jnp.float32), axis=0)


def row_order(table):
    return jnp.stack([table[0], jnp.swapaxes(table[1], 0, 1)], axis=2)


def plane_tables(expert):
    x, y, core = expert // (SIDE * CORES), (expert // CORES) % SIDE, expert % CORES
    a = jnp.where(core == 0, x, y)
    b = jnp.where(core == 0, y, x)
    step = jnp.arange(SIDE, dtype=jnp.int32)

    def index(c, outer, inner):
        outer = outer % SIDE
        inner = inner % SIDE
        even = (outer * SIDE + inner) * CORES
        odd = (inner * SIDE + outer) * CORES + 1
        return jnp.where(c == 0, even, odd).astype(jnp.int32)

    k, j = step[:, None], step[None, :]
    back = SIDE - k, SIDE - j
    own_in = index(core, a + back[0], b + back[1])
    mate_in = index(1 - core, b + back[0], a + back[1])
    own_out = index(core, a + k, b + j)
    mate_out = index(1 - core, b + k, a + j)
    return own_in, mate_in, own_out, mate_out


def in_body(spots, fresh, table, *refs):
    count = len(spots)
    arrays = 1 + max(a for a, _, _ in spots)
    blocks, refs = refs[:arrays], refs[arrays:]
    sources, gains = refs[:2], refs[2 : 2 + count]
    refs = refs[2 + count :]
    acc_ref, sq_ref, left, right, held, sems = refs[-6:]
    half, depth = sources[0].shape[1:]
    step = PADDED

    @pl.when(pl.program_id(0) == 0)
    def _():
        copies = []
        for c, (_, _, (m, k, j)) in enumerate(spots):
            for side in range(2):
                source = sources[side].at[table[m, k, j]]
                copy = pltpu.make_async_copy(source, held.at[c, side], sems.at[c, side])
                copy.start()
                copies.append(copy)
        for copy in copies:
            copy.wait()
        for c in range(count):
            low, edge, high = c * step, c * step + depth, (c + 1) * step
            left[:half, low:edge] = held[c, 0]
            left[half:, low:edge] = held[c, 1]
            left[:, edge:high] = jnp.zeros((2 * half, step - depth), left.dtype)
            right[edge:high] = jnp.zeros((step - depth, right.shape[1]), right.dtype)

    square_sum = jnp.zeros(sq_ref.shape, jnp.float32) if fresh else refs[1][...]
    for c, (a, row, _) in enumerate(spots):
        wide = blocks[a][row].astype(jnp.float32)
        square_sum += jnp.sum((wide * wide).reshape(-1, 8, wide.shape[1]), axis=0)
        column = gains[c][0].T[:, :1]
        right[c * step : c * step + depth] = (wide * column).astype(right.dtype)
    sq_ref[...] = square_sum
    made = jnp.dot(left[...], right[...], preferred_element_type=jnp.float32)
    acc_ref[...] = made if fresh else made + refs[0][...]


ROW_TILE = 256


def project_in(spots, table, blocks, gate, up, gain, sums):
    count = len(spots)
    depth, rows = blocks[0].shape[1:]
    units = gate.shape[1]
    step = PADDED
    keep = pl.BlockSpec((2 * units, ROW_TILE), lambda i, t: (0, i))
    keep_sq = pl.BlockSpec((8, ROW_TILE), lambda i, t: (0, i))

    def picked(shape):
        return [
            pl.BlockSpec((1,) + shape, lambda i, t, m=m, k=k, j=j: (t[m, k, j], 0, 0))
            for _, _, (m, k, j) in spots
        ]

    in_specs = [
        pl.BlockSpec((b.shape[0], depth, ROW_TILE), lambda i, t: (0, 0, i)) for b in blocks
    ]
    in_specs += [pl.BlockSpec(memory_space=pltpu.HBM)] * 2 + picked((8, depth))
    args = [table] + list(blocks) + [gate, up] + [gain] * count
    if sums is not None:
        in_specs += [keep, keep_sq]
        args += list(sums)
    return pl.pallas_call(
        functools.partial(in_body, spots, sums is None),
        out_shape=(
            jax.ShapeDtypeStruct((2 * units, rows), jnp.float32),
            jax.ShapeDtypeStruct((8, rows), jnp.float32),
        ),
        grid_spec=pltpu.PrefetchScalarGridSpec(
            num_scalar_prefetch=1,
            grid=(rows // ROW_TILE,),
            in_specs=in_specs,
            out_specs=(keep, keep_sq),
            scratch_shapes=[
                pltpu.VMEM((2 * units, count * step), jnp.bfloat16),
                pltpu.VMEM((count * step, ROW_TILE), jnp.bfloat16),
                pltpu.VMEM((count, 2, units, depth), jnp.bfloat16),
                pltpu.SemaphoreType.DMA((count, 2)),
            ],
        ),
        compiler_params=pltpu.CompilerParams(vmem_limit_bytes=46 * 2**20),
        cost_estimate=pl.CostEstimate(
            flops=4 * count * depth * rows * units,
            bytes_accessed=2 * count * depth * (rows + 2 * units),
            transcendentals=0,
        ),
    )(*args)


def out_body(table, act_ref, scale_ref, w_ref, out_ref):
    made = jnp.dot(w_ref[0], act_ref[...], preferred_element_type=jnp.float32)
    out_ref[0] = (made * scale_ref[...]).astype(out_ref.dtype)


def out_add_body(table, act_ref, scale_ref, w_ref, mate_ref, far_ref, near_ref):
    made = jnp.dot(w_ref[0], act_ref[...], preferred_element_type=jnp.float32)
    made = made * scale_ref[...] + mate_ref[0].astype(jnp.float32)
    made = made.astype(far_ref.dtype)

    @pl.when(pl.program_id(0) < SIDE - 1)
    def _():
        far_ref[0] = made

    @pl.when(pl.program_id(0) == SIDE - 1)
    def _():
        near_ref[...] = made


def project_out(k, table, act, scale, weights, mate=None):
    units, rows = act.shape
    depth = weights.shape[1]
    block = pl.BlockSpec((1, depth, rows), lambda i, t: (i, 0, 0))
    in_specs = [
        pl.BlockSpec((units, rows), lambda i, t: (0, 0)),
        pl.BlockSpec((1, rows), lambda i, t: (0, 0)),
        pl.BlockSpec((1, depth, units), lambda i, t: (t[k, (i + 1) % SIDE], 0, 0)),
    ]
    args = [table, act, scale, weights]
    if mate is None:
        out_shape = jax.ShapeDtypeStruct((SIDE, depth, rows), jnp.bfloat16)
        out_specs = block
    else:
        in_specs.append(block)
        args.append(mate)
        out_shape = (
            jax.ShapeDtypeStruct((SIDE - 1, depth, rows), jnp.bfloat16),
            jax.ShapeDtypeStruct((depth, rows), jnp.bfloat16),
        )
        out_specs = (
            pl.BlockSpec((1, depth, rows), lambda i, t: (jnp.minimum(i, SIDE - 2), 0, 0)),
            pl.BlockSpec((depth, rows), lambda i, t: (0, 0)),
        )
    return pl.pallas_call(
        out_body if mate is None else out_add_body,
        out_shape=out_shape,
        grid_spec=pltpu.PrefetchScalarGridSpec(
            num_scalar_prefetch=1, grid=(SIDE,), in_specs=in_specs, out_specs=out_specs
        ),
        compiler_params=pltpu.CompilerParams(vmem_limit_bytes=16 * 2**20),
        cost_estimate=pl.CostEstimate(
            flops=2 * SIDE * depth * rows * units,
            bytes_accessed=2 * SIDE * depth * (rows + units),
            transcendentals=0,
        ),
    )(*args)


FAR = (2, 1, 3)
PADDED = 256


def shards(
    queries,
    latent_cache_rows,
    lengths,
    value_up_weight,
    w_output,
    residual,
    norm_gain,
    routes,
    gate_values,
    capacity,
    w_gate,
    w_up,
    w_down,
):
    latent_width = value_up_weight.shape[1]
    softmax_scale = (NOPE + ROTARY_CHANNELS) ** (-0.5)
    scores = (
        jnp.einsum("rhc,rpc->rhp", queries, latent_cache_rows, preferred_element_type=jnp.float32)
        * softmax_scale
    )
    slot_total = latent_cache_rows.shape[1]
    live_slot = lax.broadcasted_iota(jnp.int32, (1, 1, slot_total), 2) < lengths[:, None, None]
    scores = jnp.where(live_slot, scores, -jnp.inf)
    row_peak = jnp.max(scores, axis=-1, keepdims=True)
    weight_exp = jnp.exp(scores - row_peak)
    attention_probs = (weight_exp / jnp.sum(weight_exp, axis=-1, keepdims=True)).astype(
        jnp.bfloat16
    )
    latent_rows = jnp.einsum(
        "onq,oqv->onv",
        attention_probs,
        latent_cache_rows[:, :, :latent_width],
        preferred_element_type=jnp.float32,
    ).astype(jnp.bfloat16)
    head_out = jnp.einsum(
        "rhc,hcv->rhv", latent_rows, value_up_weight, preferred_element_type=jnp.float32
    ).astype(jnp.bfloat16)
    head_rows = head_out.reshape(head_out.shape[0], -1)

    expert = lax.axis_index("expert")
    layer = lax.axis_index("tensor")
    layers = lax.axis_size("tensor")
    row_total, column_width = residual.shape
    own_rows = row_total // layers
    model_width = norm_gain.shape[0]
    hidden = w_gate.shape[2]

    named = routes == expert
    member = jnp.any(named, axis=1)
    gate_of = jnp.sum(jnp.where(named, gate_values, 0.0), axis=1)
    earlier = jnp.arange(row_total)[:, None] > jnp.arange(row_total)[None, :]
    position = jnp.dot(
        earlier.astype(jnp.bfloat16),
        member.astype(jnp.bfloat16),
        preferred_element_type=jnp.float32,
    )
    limit = capacity[expert].astype(jnp.float32)
    row_weight = jnp.where(position < limit, gate_of, 0.0)

    gain = norm_gain.reshape(-1, 1, column_width)
    gain = jnp.broadcast_to(gain, (gain.shape[0], 8, column_width))

    def turned(table):
        return jnp.swapaxes(table.reshape(-1, column_width, hidden), 1, 2)

    gate, up = turned(w_gate[0]), turned(w_up[0])
    down = w_down[0].T.reshape(-1, column_width, hidden)
    own_in, mate_in, own_out, mate_out = plane_tables(expert)

    heads = gather_plane(head_rows)
    partial_out = jnp.dot(
        heads.reshape(row_total, -1), w_output, preferred_element_type=jnp.float32
    )
    partial_out = partial_out.reshape(CORES, SIDE, SIDE, -1, column_width)
    partial_out = row_order(partial_out).reshape(layers, own_rows, column_width)
    parts = lax.all_to_all(partial_out.astype(jnp.bfloat16), "tensor", 0, 0, tiled=True)
    parts, gate, up = lax.optimization_barrier((parts, gate, up))
    attention = add_blocks(parts)
    own_residual = lax.dynamic_slice_in_dim(residual, layer * own_rows, own_rows, 0)
    stream = (own_residual.astype(jnp.float32) + attention).astype(jnp.bfloat16)
    columns = lax.all_to_all(
        jnp.broadcast_to(stream[None], (layers,) + stream.shape), "tensor", 0, 0, tiled=True
    )
    held = columns, down, gain, row_weight, own_in, mate_in, own_out, mate_out
    held = lax.optimization_barrier(held)
    columns, down, gain, row_weight, own_in, mate_in, own_out, mate_out = held
    columns = columns.reshape(row_total, column_width).T

    inner = []
    for k in range(1, SIDE):
        inner.append(shift(columns, INNER, k))
    first, second = {}, {}
    for k in FAR:
        first[k] = shift(columns, OUTER, k)
    inner = jnp.stack(inner)
    for k in FAR:
        second[k] = shift(inner, OUTER, k)

    def swap(block):
        return shift(block, PAIRS, 1)

    def add_in(spots, blocks, sums):
        return project_in(spots, tables_in, blocks, gate, up, gain, sums)

    tables_in = jnp.stack([own_in, mate_in])

    def here(m, a):
        lone = ((a, 0, (m, 0, 0)),)
        return lone + tuple((a + 1, j - 1, (m, 0, j)) for j in range(1, SIDE))

    def ones(m, a):
        return tuple((a, k - 1, (m, k, 0)) for k in range(1, SIDE))

    def rest(m, a, k):
        return tuple((a, j - 1, (m, k, j)) for j in range(1, SIDE))

    blocks = [columns[None], inner, swap(columns)[None], swap(inner)]
    heads_of = jnp.stack([first[k] for k in range(1, SIDE)])
    blocks += [heads_of, swap(heads_of)]
    spots = here(0, 0) + here(1, 2) + ones(0, 4) + ones(1, 5)
    sums = add_in(spots, blocks, None)
    second[2], sums = lax.optimization_barrier((second[2], sums))
    blocks = [second[2], swap(second[2])]
    sums = add_in(rest(0, 0, 2) + rest(1, 1, 2), blocks, sums)
    second[1], second[3], sums = lax.optimization_barrier((second[1], second[3], sums))
    blocks = [second[1], second[3]]
    blocks += [swap(second[1]), swap(second[3])]
    spots = rest(0, 0, 1) + rest(0, 1, 3) + rest(1, 2, 1) + rest(1, 3, 3)
    sums = add_in(spots, blocks, sums)
    total, squares = sums
    mean_square = jnp.sum(squares, axis=0, keepdims=True) / model_width
    pre = total * lax.rsqrt(mean_square + epsilon)
    activated = (jax.nn.silu(pre[:hidden]) * pre[hidden:]).astype(jnp.bfloat16)

    scale = row_weight[None, :]

    def for_mate(k):
        made = project_out(k, mate_out, activated, scale, down)
        return shift(made, PAIRS, 1)

    far, near, mates = {}, {}, {2: for_mate(2)}
    for k, following in ((2, 1), (1, 3), (3, 0), (0, None)):
        if following is not None:
            mates[following] = for_mate(following)
        group = project_out(k, own_out, activated, scale, down, mates[k])
        if following is not None:
            far[k], near[k], activated = lax.optimization_barrier((*group, activated))
        else:
            far[k], near[k] = group
    for k in FAR:
        far[k] = shift(far[k], OUTER, k)
    for k in FAR:
        near[k] = shift(near[k], OUTER, k)
    parts = add_blocks(jnp.stack([far[k] for k in range(SIDE)])).astype(jnp.bfloat16)
    around = []
    for k in range(1, SIDE):
        around.append(shift(parts[k - 1], INNER, k))
    parts = add_blocks(jnp.stack([near[k] for k in range(SIDE)]))
    parts = (parts + add_blocks(jnp.stack(around))).astype(jnp.bfloat16)
    parts = parts.T.reshape(layers, own_rows, column_width)
    combined = add_blocks(lax.all_to_all(parts, "tensor", 0, 0, tiled=True))
    return (stream.astype(jnp.float32) + combined).astype(jnp.bfloat16)


def solution(mesh):
    in_specs = (
        P("expert", "tensor", None),
        P("expert", None, None),
        P("expert"),
        P("tensor", None, None),
        P("tensor", "expert"),
        P(None, "expert"),
        P(),
        P(),
        P(),
        P(),
        P("expert", None, "tensor"),
        P("expert", None, "tensor"),
        P("expert", "tensor", None),
    )
    out_specs = P("tensor", "expert")
    return jax.shard_map(
        shards, mesh=mesh, in_specs=in_specs, out_specs=out_specs, check_vma=False
    )
```
